32 devices in a mesh: fsdp: 8 (over y, x, core), tp: 4 (over z).
Axes of the slice: x: 2, y: 2, z: 4, core: 2. Of those that a mesh axis runs over, the one named last changes fastest.
Arguments:
- hidden_in: bfloat16 [16384, 768], P(('fsdp', 'tp')), may hold values from -6 to 6
- memory: bfloat16 [8192, 768], P(('fsdp', 'tp')), may hold values from -6 to 6
- seg_lengths: int32 [16, 7], P('fsdp'), may hold values from 1 to 1018, as said below
- seg_parents: int32 [16, 7], P('fsdp'), may hold values from 0 to 5, as said below
- path_pos: int32 [16384], P('fsdp'), may hold values from 0 to 1023, as said below
- self_query: bfloat16 [768, 768], P('fsdp', 'tp'), may hold values from -0.0546875 to 0.0546875
- self_key: bfloat16 [768, 768], P('fsdp', 'tp'), may hold values from -0.21875 to 0.21875
- self_value: bfloat16 [768, 768], P('fsdp', 'tp'), may hold values from -0.21875 to 0.21875
- self_output: bfloat16 [768, 768], P('tp', 'fsdp'), may hold values from -0.625 to 0.625
- attn_gain: bfloat16 [768], P('fsdp'), may hold values from 0.5 to 1.5
- cross_query: bfloat16 [768, 768], P('fsdp', 'tp'), may hold values from -0.0546875 to 0.0546875
- cross_key: bfloat16 [768, 768], P('fsdp', 'tp'), may hold values from -0.21875 to 0.21875
- cross_value: bfloat16 [768, 768], P('fsdp', 'tp'), may hold values from -0.21875 to 0.21875
- cross_output: bfloat16 [768, 768], P('tp', 'fsdp'), may hold values from -0.75 to 0.75
- cross_gain: bfloat16 [768], P('fsdp'), may hold values from 0.5 to 1.5
- gate_weight: bfloat16 [768, 2048], P('fsdp', 'tp'), may hold values from -0.21875 to 0.21875
- up_weight: bfloat16 [768, 2048], P('fsdp', 'tp'), may hold values from -0.21875 to 0.21875
- down_weight: bfloat16 [2048, 768], P('tp', 'fsdp'), may hold values from -0.125 to 0.125
- feed_gain: bfloat16 [768], P('fsdp'), may hold values from 0.5 to 1.5
- out_grad: bfloat16 [16384, 768], P(('fsdp', 'tp')), may hold values from -6 to 6
Outputs:
- layer_out: bfloat16 [16384, 768], P(('fsdp', 'tp'))
- input_grad: float32 [16384, 768], P(('fsdp', 'tp'))
- memory_grad: float32 [8192, 768], P(('fsdp', 'tp'))
- grad_self_query: float32 [768, 768], P('fsdp', 'tp')
- grad_self_key: float32 [768, 768], P('fsdp', 'tp')
- grad_self_value: float32 [768, 768], P('fsdp', 'tp')
- grad_self_output: float32 [768, 768], P('tp', 'fsdp')
- grad_attn_gain: float32 [768], P('fsdp')
- grad_cross_query: float32 [768, 768], P('fsdp', 'tp')
- grad_cross_key: float32 [768, 768], P('fsdp', 'tp')
- grad_cross_value: float32 [768, 768], P('fsdp', 'tp')
- grad_cross_output: float32 [768, 768], P('tp', 'fsdp')
- grad_cross_gain: float32 [768], P('fsdp')
- grad_gate_weight: float32 [768, 2048], P('fsdp', 'tp')
- grad_up_weight: float32 [768, 2048], P('fsdp', 'tp')
- grad_down_weight: float32 [2048, 768], P('tp', 'fsdp')
- grad_feed_gain: float32 [768], P('fsdp')
The draws below stay inside these ranges and needn't reach their ends.
Inputs may be any that keep to these rules, and one draw needn't show every extreme that they name: `seg_lengths`: each tree's lengths sum to 1024; its segments lie in the order of their numbers. `seg_parents`: segment 0 is its own parent; the parent of segment k > 0 is an earlier segment. `path_pos`: A token's position is its offset in its segment plus the lengths of all of its segment's ancestors other than itself.
All inputs are finite; a program needn't handle non-finite values.
Results may differ from the reference program's by a relative error of at most 0.029.
Values may be sent and summed in bfloat16 or wider, within the bound.
No kernel may reach another device: no remote copies, remote signals or barrier semaphores. Data moves between devices by JAX's collectives and lax.ppermute only.
A program may use at most 128 MiB of HBM per device.

```python
import jax
import jax.numpy as jnp
from jax import lax

D = 768
HEADS = 12
HEAD_DIM = 64
FF = 2048
INNER = 768
SEGS = 7
TREE = 1024
MEM = 512
TREES = 16


def tree_shapes(key):
    base = jax.random.fold_in(key, 7001)
    keys = jax.random.split(base, TREES)
    numbers = jnp.arange(TREES, dtype=jnp.int32)

    def one_tree(subkey, number):
        cut_key, parent_key = jax.random.split(subkey)
        order = jax.random.permutation(cut_key, TREE - 1)[:SEGS - 1] + 1
        cuts = jnp.sort(order).astype(jnp.int32)
        chain_cuts = jnp.arange(1, SEGS, dtype=jnp.int32)
        cuts = jnp.where(number == 0, chain_cuts, cuts)
        bounds = jnp.concatenate([jnp.zeros((1,), jnp.int32), cuts, jnp.full((1,), TREE, jnp.int32)])
        lengths = bounds[1:] - bounds[:-1]
        labels = jnp.arange(SEGS, dtype=jnp.int32)
        raw = jax.random.randint(parent_key, (SEGS,), 0, 1 << 20)
        parents = jnp.where(labels > 0, raw % jnp.maximum(labels, 1), 0).astype(jnp.int32)
        chain = jnp.maximum(labels - 1, 0)
        parents = jnp.where(number == 0, chain, parents).astype(jnp.int32)
        return (lengths.astype(jnp.int32), parents)
    return jax.vmap(one_tree)(keys, numbers)


def draw_seg_lengths(key, part):
    return tree_shapes(key)[0]


def draw_seg_parents(key, part):
    return tree_shapes(key)[1]


def draw_path_pos(key, part):
    lengths, parents = tree_shapes(key)

    def one_tree(lengths, parents):
        labels = jnp.arange(SEGS, dtype=jnp.int32)
        parent_of = (parents[:, None] == labels[None, :]).astype(jnp.int32)
        current = jnp.eye(SEGS, dtype=jnp.int32)
        above = jnp.zeros((SEGS, SEGS), jnp.int32)
        for level in range(SEGS - 1):
            current = jnp.dot(current, parent_of)
            above = jnp.maximum(above, current)
        above = jnp.minimum(above, 1) * (1 - jnp.eye(SEGS, dtype=jnp.int32))
        before = jnp.dot(above, lengths)
        starts = jnp.cumsum(lengths) - lengths
        spots = jnp.arange(TREE, dtype=jnp.int32)
        segment = jnp.sum((spots[:, None] >= jnp.cumsum(lengths)[None, :-1]).astype(jnp.int32), axis=1)
        member = (segment[:, None] == labels[None, :]).astype(jnp.int32)
        return spots - jnp.dot(member, starts) + jnp.dot(member, before)
    return jax.vmap(one_tree)(lengths, parents).reshape(-1).astype(jnp.int32)


def raised(values, key, source, target, shards_of, factor):
    def block_of(dim):
        return (jnp.arange(values.shape[dim]) // (values.shape[dim] // shards_of)).reshape((-1,) + (1,) * (values.ndim - 1 - dim))

    first = jax.random.permutation(key, shards_of)[block_of(target)]
    far = (block_of(target) + shards_of // 2) % shards_of
    return jnp.where((block_of(source) == first) | (block_of(source) == far), factor * values, values)


def shard_levels(own_key, dims, cuts, low, top_value):
    loudness = 1.0
    for position, shards_of in cuts:
        heights = jax.random.uniform(jax.random.fold_in(jax.random.fold_in(own_key, 6), position), (shards_of,), jnp.float32, low / len(cuts), top_value / len(cuts))
        loudness = loudness * jnp.repeat(jnp.exp(heights), dims[position] // shards_of).reshape((-1,) + (1,) * (len(dims) - 1 - position))
    return loudness


def gaussian(rng, dims, scale, bound, pieces=(), kind=jnp.bfloat16):
    level = shard_levels(rng, dims, pieces, -0.22, 0.18) if pieces else 1.0
    drawn = jax.random.normal(rng, dims, jnp.float32) * scale * level
    return jnp.minimum(jnp.maximum(drawn, -bound), bound).astype(kind)


def heavy_noise(rng, shape, width, most, shards, heavy, kind=jnp.bfloat16):
    values = width * jax.random.normal(rng, shape, jnp.float32)
    if shards:
        values = values * shard_levels(rng, shape, shards, -0.22, 0.18)
    return jnp.clip(raised(values, jax.random.fold_in(rng, 3), *heavy), -most, most).astype(kind)


def setup_inputs(seed: int = 0) -> dict:
    key_list = jax.random.split(jax.random.key(seed), 21)
    return {
        "hidden_in": heavy_noise(key_list[0], (TREES * TREE, D), 1.0, 6.0, ((0, 32),), (0, 1, 32, 2.75)),
        "memory": gaussian(key_list[1], (TREES * MEM, D), 1.0, 6.0, ((0, 32),)),
        "seg_lengths": draw_seg_lengths(jax.random.fold_in(key_list[20], 71), 0),
        "seg_parents": draw_seg_parents(jax.random.fold_in(key_list[20], 71), 0),
        "path_pos": draw_path_pos(jax.random.fold_in(key_list[20], 71), 0),
        "self_query": gaussian(key_list[5], (D, INNER), (D * 16) ** -0.5, 0.0546875, ((0, 8), (1, 4))),
        "self_key": gaussian(key_list[6], (D, INNER), D ** -0.5, 0.21875, ((0, 8), (1, 4))),
        "self_value": gaussian(key_list[7], (D, INNER), D ** -0.5, 0.21875, ((0, 8), (1, 4))),
        "self_output": gaussian(key_list[8], (INNER, D), (INNER // 8) ** -0.5, 0.625, ((0, 4), (1, 8))),
        "attn_gain": jnp.clip(1.0 + 0.1 * jax.random.normal(key_list[9], (D,), jnp.float32), 0.5, 1.5).astype(jnp.bfloat16),
        "cross_query": gaussian(key_list[10], (D, INNER), (D * 16) ** -0.5, 0.0546875, ((0, 8), (1, 4))),
        "cross_key": gaussian(key_list[11], (D, INNER), D ** -0.5, 0.21875, ((0, 8), (1, 4))),
        "cross_value": gaussian(key_list[12], (D, INNER), D ** -0.5, 0.21875, ((0, 8), (1, 4))),
        "cross_output": gaussian(key_list[13], (INNER, D), (INNER // 12) ** -0.5, 0.75, ((0, 4), (1, 8))),
        "cross_gain": jnp.clip(1.0 + 0.1 * jax.random.normal(key_list[14], (D,), jnp.float32), 0.5, 1.5).astype(jnp.bfloat16),
        "gate_weight": gaussian(key_list[15], (D, FF), D ** -0.5, 0.21875, ((0, 8), (1, 4))),
        "up_weight": gaussian(key_list[16], (D, FF), D ** -0.5, 0.21875, ((0, 8), (1, 4))),
        "down_weight": gaussian(key_list[17], (FF, D), FF ** -0.5, 0.125, ((0, 4), (1, 8))),
        "feed_gain": jnp.clip(1.0 + 0.1 * jax.random.normal(key_list[18], (D,), jnp.float32), 0.5, 1.5).astype(jnp.bfloat16),
        "out_grad": heavy_noise(key_list[19], (TREES * TREE, D), 1.0, 6.0, ((0, 32),), (0, 1, 32, 2.75)),
    }


EPS = 1e-06
HIGH = lax.Precision.HIGHEST

@jax.custom_vjp
def low(v):
    return lax.optimization_barrier(v.astype(jnp.bfloat16)).astype(jnp.float32)

@jax.custom_vjp
def low_back(v):
    return v

def low_keep(v):
    return (low(v), None)

def low_pass(kept, grad):
    return (grad,)

def back_keep(v):
    return (v, None)

def back_low(kept, grad):
    return (low(grad),)
low.defvjp(low_keep, low_pass)
low_back.defvjp(back_keep, back_low)

def both_ways(values):
    return low(low_back(values))

def matmul(left, right):
    return jnp.dot(left, right, precision=HIGH, preferred_element_type=jnp.float32)

def rms_norm(values, gain):
    return values * lax.rsqrt(lax.optimization_barrier(jnp.mean(values * values, axis=-1, keepdims=True)) + EPS) * gain

def tree_mask(lengths, parents, places):
    count = lengths.shape[0]
    spots = jnp.arange(places.shape[0], dtype=jnp.int32)
    bounds = jnp.cumsum(lengths)[:-1]
    segment = lax.optimization_barrier(jnp.sum((spots[:, None] >= bounds[None, :]).astype(jnp.int32), axis=1))
    labels = jnp.arange(count, dtype=jnp.int32)
    member = (segment[:, None] == labels[None, :]).astype(jnp.float32)
    parent_of = (parents[:, None] == labels[None, :]).astype(jnp.float32)
    current = jnp.eye(count, dtype=jnp.float32)
    above = current
    for level in range(count - 1):
        current = jnp.dot(current, parent_of, precision=HIGH)
        above = jnp.maximum(above, current)
    reach = jnp.dot(jnp.dot(member, above, precision=HIGH), member.T, precision=HIGH)
    return (reach > 0.5) & (places[None, :] <= places[:, None])

def attend(query, key, value, mask):
    heads = query.reshape(query.shape[0], HEADS, HEAD_DIM)
    keys = key.reshape(key.shape[0], HEADS, HEAD_DIM)
    values = value.reshape(value.shape[0], HEADS, HEAD_DIM)
    scores = low_back(jnp.einsum('qhd,khd->hqk', heads, keys, precision=HIGH))
    scores = jnp.where(mask[None], scores, -1e+30)
    weights = low(jax.nn.softmax(scores, axis=-1))
    mixed = jnp.einsum('hqk,khd->qhd', weights, values, precision=HIGH)
    return mixed.reshape(query.shape[0], HEADS * HEAD_DIM)

def reference(hidden_in, memory, seg_lengths, seg_parents, path_pos, self_query, self_key, self_value, self_output, attn_gain, cross_query, cross_key, cross_value, cross_output, cross_gain, gate_weight, up_weight, down_weight, feed_gain, out_grad):
    places = path_pos.reshape(-1, TREE)

    def self_tree(parts):
        query, key, value, lengths, parents, spots = parts
        return attend(query, key, value, tree_mask(lengths, parents, spots))

    def cross_tree(parts):
        query, key, value = parts
        return attend(query, key, value, jnp.ones((query.shape[0], key.shape[0]), dtype=jnp.bool_))

    def layer(resid, source, self_query, self_key, self_value, self_output, attn_gain, cross_query, cross_key, cross_value, cross_output, cross_gain, gate_weight, up_weight, down_weight, feed_gain):
        normed = low(rms_norm(resid, attn_gain))
        query = both_ways(matmul(normed, self_query))
        key = both_ways(matmul(normed, self_key))
        value = both_ways(matmul(normed, self_value))
        mixed = lax.map(jax.checkpoint(self_tree), (query.reshape(-1, TREE, INNER), key.reshape(-1, TREE, INNER), value.reshape(-1, TREE, INNER), seg_lengths, seg_parents, places))
        mixed = both_ways(mixed.reshape(-1, INNER))
        after_attn = resid + low_back(matmul(mixed, self_output))
        normed = low(rms_norm(after_attn, cross_gain))
        query = both_ways(matmul(normed, cross_query))
        key = both_ways(matmul(source, cross_key))
        value = both_ways(matmul(source, cross_value))
        mixed = lax.map(jax.checkpoint(cross_tree), (query.reshape(-1, TREE, INNER), key.reshape(-1, MEM, INNER), value.reshape(-1, MEM, INNER)))
        mixed = both_ways(mixed.reshape(-1, INNER))
        after_cross = after_attn + low_back(matmul(mixed, cross_output))
        normed = low(rms_norm(after_cross, feed_gain))
        gate = low_back(matmul(normed, gate_weight))
        up = low_back(matmul(normed, up_weight))
        inner = low(jax.nn.gelu(gate, approximate=True) * up)
        return after_cross + low_back(matmul(inner, down_weight))
    floats = tuple((v.astype(jnp.float32) for v in (hidden_in, memory, self_query, self_key, self_value, self_output, attn_gain, cross_query, cross_key, cross_value, cross_output, cross_gain, gate_weight, up_weight, down_weight, feed_gain)))
    result, pullback = jax.vjp(layer, *floats)
    grads = pullback(out_grad.astype(jnp.float32))
    return (result.astype(jnp.bfloat16), grads[0], grads[1], grads[2], grads[3], grads[4], grads[5], grads[6], grads[7], grads[8], grads[9], grads[10], grads[11], grads[12], grads[13], grads[14], grads[15])
```

```python
import functools

import jax
import jax.numpy as jnp
from jax import lax
from jax.experimental import pallas as pl
from jax.experimental.pallas import tpu as pltpu
from jax.sharding import PartitionSpec as P


HEAD = 64
EPS = 1e-06
NEG = -1e30
BF = jnp.bfloat16
F32 = jnp.float32
PIECES = 8
VMEM_LIMIT = 60 * 1024 * 1024


def nn(left, right):
    return lax.dot_general(left, right, (((1,), (0,)), ((), ())), preferred_element_type=F32)


def nt(left, right):
    return lax.dot_general(left, right, (((1,), (1,)), ((), ())), preferred_element_type=F32)


def tn(left, right):
    return lax.dot_general(left, right, (((0,), (0,)), ((), ())), preferred_element_type=F32)


def unit(values):
    scale = lax.rsqrt(jnp.mean(values * values, axis=-1, keepdims=True) + EPS)
    return values * scale, scale


def unit_back(grad, gain, normal, scale):
    inner = grad * gain
    return scale * (inner - normal * jnp.mean(inner * normal, axis=-1, keepdims=True))


def fetch_all(meta, pieces, store, sems, columns):
    def copy(t, r):
        rows = pieces[r].shape[1]
        start = pl.multiple_of(meta[r] * rows, rows)
        return pltpu.make_async_copy(
            pieces[r].at[t, :, columns], store.at[t, pl.ds(start, rows), :], sems.at[t, r]
        )

    for t in range(store.shape[0]):
        for r in range(PIECES):
            copy(t, r).start()

    def wait(t):
        for r in range(PIECES):
            copy(t, r).wait()

    return wait


def sender(meta, outs, slots, sems):
    def copy(t, r):
        rows = outs[r].shape[1]
        start = pl.multiple_of(meta[r] * rows, rows)
        return pltpu.make_async_copy(
            slots.at[lax.rem(t, 2), pl.ds(start, rows), :], outs[r].at[t], sems.at[lax.rem(t, 2), r]
        )

    def start(t):
        for r in range(PIECES):
            copy(t, r).start()

    def wait(t):
        for r in range(PIECES):
            copy(t, r).wait()

    return start, wait


def mask_columns(meta, lengths, parents, rows):
    count = lengths.shape[1]
    tree, half = meta[PIECES], meta[PIECES + 1]
    starts, bits = [], []
    total = jnp.int32(0)
    for s in range(count):
        starts.append(total)
        total = total + lengths[tree, s]
    starts.append(total)
    for s in range(count):
        if s == 0:
            bits.append(jnp.int32(1))
            continue
        above = bits[0]
        for b in range(1, s):
            above = jnp.where(parents[tree, s] == b, bits[b], above)
        bits.append(above | (1 << s))
    lane = lax.broadcasted_iota(jnp.int32, (rows, 128), 1)
    own = lax.broadcasted_iota(jnp.int32, (rows, 128), 0) + half * rows
    other = lax.broadcasted_iota(jnp.int32, (rows, 128), 0) + (1 - half) * rows
    line = lax.broadcasted_iota(jnp.int32, (1, 128), 1)
    query = jnp.zeros((rows, 128), F32)
    key_own = jnp.zeros((rows, 128), F32)
    key_other = jnp.zeros((rows, 128), F32)
    for s in range(count):
        inside = (own >= starts[s]) & (own < starts[s + 1])
        query = jnp.where(inside & (lane == HEAD + s), 1.0, query)
        barred = jnp.zeros((1, 128), F32)
        for q in range(count):
            hit = (bits[q] >> s) & 1
            barred = jnp.where(line == HEAD + q, jnp.where(hit == 1, 0.0, NEG), barred)
        key_own = jnp.where(inside, barred, key_own)
        inside = (other >= starts[s]) & (other < starts[s + 1])
        key_other = jnp.where(inside, barred, key_other)
    closed = jnp.where((line >= HEAD) & (line < HEAD + count), NEG, 0.0)
    key_other = jnp.where(half == 0, jnp.broadcast_to(closed, (rows, 128)), key_other)
    return query.astype(BF), key_own.astype(BF), key_other.astype(BF)


def joined(values, extra):
    return jnp.concatenate([values, extra[:, HEAD:]], axis=1)


def causal(size):
    row = lax.broadcasted_iota(jnp.int32, (size, size), 0)
    col = lax.broadcasted_iota(jnp.int32, (size, size), 1)
    return col <= row


def self_forward_kernel(columns, meta, lengths, parents, *refs):
    pieces = refs[:PIECES]
    own_ref, other_ref, gain_ref = refs[PIECES : PIECES + 3]
    mixed_ref, kv_ref, q_ref, lse_ref = refs[PIECES + 3 : PIECES + 7]
    weights, normed, qmask, kmask, sems = refs[PIECES + 7 :]
    rows = own_ref.shape[0]
    half_rows = rows // 2
    wait = fetch_all(meta, pieces, weights, sems, columns)
    gain = gain_ref[...]
    normed[:rows] = (unit(other_ref[...].astype(F32))[0] * gain).astype(BF)
    normed[rows:] = (unit(own_ref[...].astype(F32))[0] * gain).astype(BF)
    qm, ko, kp = mask_columns(meta, lengths, parents, rows)
    qmask[...] = qm
    kmask[:rows] = kp
    kmask[rows:] = ko
    width = mixed_ref.shape[2]
    lane = lax.broadcasted_iota(jnp.int32, (rows, 128), 1)

    def block(t, carry):
        wait(t)
        kv_ref[t] = nn(normed[...], weights[t, :, : 2 * width]).astype(BF)
        q_ref[t] = nn(normed[rows:], weights[t, :, 2 * width :]).astype(BF)
        lse = jnp.zeros((rows, 128), F32)
        for h in range(width // HEAD):
            at = slice(h * HEAD, (h + 1) * HEAD)
            qc = joined(q_ref[t, :, at], qmask[...])
            kc = joined(kv_ref[t, :, at], kmask[...])
            v = kv_ref[t, :, width + h * HEAD : width + (h + 1) * HEAD]
            tops = []
            for b in range(2):
                seen = rows + b * half_rows
                queries = qc[b * half_rows : (b + 1) * half_rows]
                s0 = nt(queries, kc[:seen])
                s1 = jnp.where(causal(half_rows), nt(queries, kc[seen : seen + half_rows]), NEG)
                top = jnp.maximum(
                    jnp.max(s0, axis=1, keepdims=True), jnp.max(s1, axis=1, keepdims=True)
                )
                p0 = jnp.exp(s0 - top)
                p1 = jnp.exp(s1 - top)
                total = jnp.sum(p0, axis=1, keepdims=True) + jnp.sum(p1, axis=1, keepdims=True)
                out = nn(p0.astype(BF), v[:seen]) + nn(p1.astype(BF), v[seen : seen + half_rows])
                mixed_ref[t, b * half_rows : (b + 1) * half_rows, at] = (out / total).astype(BF)
                tops.append(top + jnp.log(total))
            lse = jnp.where(lane == h, jnp.concatenate(tops, axis=0), lse)
        lse_ref[t] = lse
        return carry

    lax.fori_loop(0, weights.shape[0], block, 0)


def cross_forward_kernel(columns, meta, *refs):
    pieces = refs[:PIECES]
    own_ref, mixed_ref, mem_ref, gain_ref = refs[PIECES : PIECES + 4]
    after_ref, cross_ref, mixed2_ref, q_ref, kv_ref, lse_ref = refs[PIECES + 4 : PIECES + 10]
    weights, normed, sems = refs[PIECES + 10 :]
    rows = own_ref.shape[0]
    width = mixed_ref.shape[2]
    wait = fetch_all(meta, pieces, weights, sems, columns)
    blocks = weights.shape[0]
    after_ref[...] = own_ref[...].astype(F32)

    def project(t, carry):
        wait(t)
        after_ref[...] += nt(mixed_ref[t], weights[t, :, 2 * width : 3 * width])
        return carry

    lax.fori_loop(0, blocks, project, 0)
    normed[...] = (unit(after_ref[...])[0] * gain_ref[...]).astype(BF)
    cross_ref[...] = after_ref[...]
    lane = lax.broadcasted_iota(jnp.int32, (rows, 128), 1)

    def block(t, carry):
        kv_ref[t] = nn(mem_ref[...], weights[t, :, : 2 * width]).astype(BF)
        q_ref[t] = nn(normed[...], weights[t, :, 3 * width : 4 * width]).astype(BF)
        lse = jnp.zeros((rows, 128), F32)
        for h in range(width // HEAD):
            at = slice(h * HEAD, (h + 1) * HEAD)
            s = nt(q_ref[t, :, at], kv_ref[t, :, at])
            top = jnp.max(s, axis=1, keepdims=True)
            p = jnp.exp(s - top)
            total = jnp.sum(p, axis=1, keepdims=True)
            out = nn(p.astype(BF), kv_ref[t, :, width + h * HEAD : width + (h + 1) * HEAD])
            mixed2_ref[t, :, at] = (out / total).astype(BF)
            lse = jnp.where(lane == h, top + jnp.log(total), lse)
        lse_ref[t] = lse
        cross_ref[...] += nt(mixed2_ref[t], weights[t, :, 4 * width :])
        return carry

    lax.fori_loop(0, blocks, block, 0)


def gelu_parts(v):
    c = 0.7978845608028654
    inner = c * (v + 0.044715 * v * v * v)
    th = jnp.tanh(inner)
    half = 0.5 * (1.0 + th)
    slope = half + 0.5 * v * (1.0 - th * th) * c * (1.0 + 3 * 0.044715 * v * v)
    return v * half, slope


def feed_kernel(columns, meta, *refs):
    pieces = refs[:PIECES]
    cross_ref, grad_ref, gain_ref = refs[PIECES : PIECES + 3]
    outs = refs[PIECES + 3 : 2 * PIECES + 3]
    out_ref, back_ref, dgain_ref = refs[2 * PIECES + 3 : 2 * PIECES + 6]
    weights, normed, normed_t, grad_t, total, back, slots, sems, out_sems = refs[2 * PIECES + 6 :]
    wait = fetch_all(meta, pieces, weights, sems, columns)
    send, drain = sender(meta, outs, slots, out_sems)
    blocks = weights.shape[0]
    hidden = weights.shape[2] // 3
    low = (unit(cross_ref[...])[0] * gain_ref[...]).astype(BF)
    normed[...] = low
    normed_t[...] = low.T
    grad_t[...] = grad_ref[...].T
    total[...] = cross_ref[...]
    back[...] = jnp.zeros_like(back)

    def block(t, carry):
        wait(t)
        gate = nn(normed[...], weights[t, :, :hidden])
        up = nn(normed[...], weights[t, :, hidden : 2 * hidden])
        act, slope = gelu_parts(gate)
        inner = (act * up).astype(BF)
        total[...] += nt(inner, weights[t, :, 2 * hidden :])
        grad_inner = nn(grad_ref[...], weights[t, :, 2 * hidden :])
        grad_gate = (grad_inner * up * slope).astype(BF)
        grad_up = (grad_inner * act).astype(BF)
        back[...] += nt(grad_gate, weights[t, :, :hidden]) + nt(
            grad_up, weights[t, :, hidden : 2 * hidden]
        )

        @pl.when(t >= 2)
        def _():
            drain(t - 2)

        slot = lax.rem(t, 2)
        slots[slot, :, :hidden] = nn(normed_t[...], grad_gate).astype(BF)
        slots[slot, :, hidden : 2 * hidden] = nn(normed_t[...], grad_up).astype(BF)
        slots[slot, :, 2 * hidden :] = nn(grad_t[...], inner).astype(BF)
        send(t)
        return carry

    lax.fori_loop(0, blocks, block, 0)
    out_ref[...] = total[...].astype(BF)
    normal, scale = unit(cross_ref[...])
    gain = gain_ref[...]
    dgain_ref[...] = jnp.sum(back[...] * normal, axis=0, keepdims=True)
    back_ref[...] = grad_ref[...].astype(F32) + unit_back(back[...], gain, normal, scale)
    drain(blocks - 2)
    drain(blocks - 1)


def cross_backward_kernel(columns, meta, *refs):
    pieces = refs[:PIECES]
    (grad_ref, after_ref, mem_ref, gain_ref, mixed_ref, q_ref, kv_ref, lse_ref) = refs[
        PIECES : PIECES + 8
    ]
    outs = refs[PIECES + 8 : 2 * PIECES + 8]
    back_ref, dmem_ref, dgain_ref = refs[2 * PIECES + 8 : 2 * PIECES + 11]
    (weights, normed_t, grad_low, grad_t, mem_t, back, dmem, dq, dkv, slots, sems, out_sems) = refs[
        2 * PIECES + 11 :
    ]
    wait = fetch_all(meta, pieces, weights, sems, columns)
    send, drain = sender(meta, outs, slots, out_sems)
    blocks = weights.shape[0]
    width = mixed_ref.shape[2]
    gain = gain_ref[...]
    normed_t[...] = (unit(after_ref[...])[0] * gain).astype(BF).T
    low = grad_ref[...].astype(BF)
    grad_low[...] = low
    grad_t[...] = low.T
    mem_t[...] = mem_ref[...].T
    back[...] = jnp.zeros_like(back)
    dmem[...] = jnp.zeros_like(dmem)

    def block(t, carry):
        wait(t)
        grad_mixed = nn(grad_low[...], weights[t, :, 4 * width :]).astype(BF)
        for h in range(width // HEAD):
            at = slice(h * HEAD, (h + 1) * HEAD)
            q = q_ref[t, :, at]
            k = kv_ref[t, :, at]
            v = kv_ref[t, :, width + h * HEAD : width + (h + 1) * HEAD]
            g = grad_mixed[:, at]
            delta = jnp.sum(
                g.astype(F32) * mixed_ref[t, :, at].astype(F32), axis=1, keepdims=True
            )
            p = jnp.exp(nt(q, k) - lse_ref[t, :, h : h + 1])
            ds = (p * (nt(g, v) - delta)).astype(BF)
            dq[:, at] = nn(ds, k).astype(BF)
            dkv[:, at] = tn(ds, q).astype(BF)
            dkv[:, width + h * HEAD : width + (h + 1) * HEAD] = tn(p.astype(BF), g).astype(BF)
        back[...] += nt(dq[...], weights[t, :, 3 * width : 4 * width])
        dmem[...] += nt(dkv[...], weights[t, :, : 2 * width])

        @pl.when(t >= 2)
        def _():
            drain(t - 2)

        slot = lax.rem(t, 2)
        slots[slot, :, : 2 * width] = nn(mem_t[...], dkv[...]).astype(BF)
        slots[slot, :, 2 * width : 3 * width] = nn(normed_t[...], dq[...]).astype(BF)
        slots[slot, :, 3 * width :] = nn(grad_t[...], mixed_ref[t]).astype(BF)
        send(t)
        return carry

    lax.fori_loop(0, blocks, block, 0)
    normal, scale = unit(after_ref[...])
    dgain_ref[...] = jnp.sum(back[...] * normal, axis=0, keepdims=True)
    back_ref[...] = grad_ref[...] + unit_back(back[...], gain, normal, scale)
    dmem_ref[...] = dmem[...].astype(BF)
    drain(blocks - 2)
    drain(blocks - 1)


def self_backward_kernel(columns, columns_out, meta, lengths, parents, *refs):
    pieces = refs[:PIECES]
    pieces_out = refs[PIECES : 2 * PIECES]
    base = 2 * PIECES
    (grad_ref, own_ref, other_ref, gain_ref, mixed_ref, q_ref, kv_ref, lse_ref) = refs[
        base : base + 8
    ]
    outs = refs[base + 8 : base + 8 + PIECES]
    base = base + 8 + PIECES
    back_ref, away_ref, dgain_ref = refs[base : base + 3]
    (
        weights,
        weights_out,
        normed_t,
        grad_low,
        grad_t,
        back,
        dq,
        dkv,
        qmask,
        kmask,
        slots,
        sems,
        sems_o,
        out_sems,
    ) = refs[base + 3 :]
    wait = fetch_all(meta, pieces, weights, sems, columns)
    wait_out = fetch_all(meta, pieces_out, weights_out, sems_o, columns_out)
    send, drain = sender(meta, outs, slots, out_sems)
    blocks = weights.shape[0]
    width = mixed_ref.shape[2]
    rows = own_ref.shape[0]
    half_rows = rows // 2
    gain = gain_ref[...]
    normed_t[:, :rows] = (unit(other_ref[...].astype(F32))[0] * gain).astype(BF).T
    normed_t[:, rows:] = (unit(own_ref[...].astype(F32))[0] * gain).astype(BF).T
    low = grad_ref[...].astype(BF)
    grad_low[...] = low
    grad_t[...] = low.T
    qm, ko, kp = mask_columns(meta, lengths, parents, rows)
    qmask[...] = qm
    kmask[:rows] = kp
    kmask[rows:] = ko
    back[...] = jnp.zeros_like(back)

    def block(t, carry):
        wait(t)
        wait_out(t)
        grad_mixed = nn(grad_low[...], weights_out[t, :, :width]).astype(BF)
        for h in range(width // HEAD):
            at = slice(h * HEAD, (h + 1) * HEAD)
            q = q_ref[t, :, at]
            k = kv_ref[t, :, at]
            v = kv_ref[t, :, width + h * HEAD : width + (h + 1) * HEAD]
            qc = joined(q, qmask[...])
            kc = joined(k, kmask[...])
            g = grad_mixed[:, at]
            delta = jnp.sum(
                g.astype(F32) * mixed_ref[t, :, at].astype(F32), axis=1, keepdims=True
            )
            lse = lse_ref[t, :, h : h + 1]
            dk_parts = [None] * 3
            dv_parts = [None] * 3
            spans = ((0, rows), (rows, rows + half_rows), (rows + half_rows, 2 * rows))
            for b in range(2):
                mine = slice(b * half_rows, (b + 1) * half_rows)
                dq_sum = None
                for part in range(b + 2):
                    lo, hi = spans[part]
                    s = nt(qc[mine], kc[lo:hi])
                    if part == b + 1:
                        s = jnp.where(causal(half_rows), s, NEG)
                    p = jnp.exp(s - lse[mine])
                    ds = (p * (nt(g[mine], v[lo:hi]) - delta[mine])).astype(BF)
                    add = nn(ds, k[lo:hi])
                    dq_sum = add if dq_sum is None else dq_sum + add
                    add_k = tn(ds, q[mine])
                    add_v = tn(p.astype(BF), g[mine])
                    dk_parts[part] = add_k if dk_parts[part] is None else dk_parts[part] + add_k
                    dv_parts[part] = add_v if dv_parts[part] is None else dv_parts[part] + add_v
                dq[mine, at] = dq_sum.astype(BF)
            for part in range(3):
                lo, hi = spans[part]
                dkv[lo:hi, at] = dk_parts[part].astype(BF)
                dkv[lo:hi, width + h * HEAD : width + (h + 1) * HEAD] = dv_parts[part].astype(BF)
        back[...] += nt(dkv[...], weights[t, :, : 2 * width])
        back[rows:] += nt(dq[...], weights[t, :, 2 * width :])

        @pl.when(t >= 2)
        def _():
            drain(t - 2)

        slot = lax.rem(t, 2)
        slots[slot, :, : 2 * width] = nn(normed_t[...], dkv[...]).astype(BF)
        slots[slot, :, 2 * width : 3 * width] = nn(normed_t[:, rows:], dq[...]).astype(BF)
        slots[slot, :, 3 * width :] = nn(grad_t[...], mixed_ref[t]).astype(BF)
        send(t)
        return carry

    lax.fori_loop(0, blocks, block, 0)
    normal = unit(other_ref[...].astype(F32))[0]
    sums = jnp.sum(back[:rows] * normal, axis=0, keepdims=True)
    normal = unit(own_ref[...].astype(F32))[0]
    dgain_ref[...] = sums + jnp.sum(back[rows:] * normal, axis=0, keepdims=True)
    away_ref[...] = back[:rows].astype(BF)
    back_ref[...] = back[rows:]
    drain(blocks - 2)
    drain(blocks - 1)


def finish_kernel(grad_ref, own_ref, back_ref, came_ref, gain_ref, out_ref):
    normal, scale = unit(own_ref[...].astype(F32))
    total = back_ref[...] + came_ref[...].astype(F32)
    out_ref[...] = grad_ref[...] + unit_back(total, gain_ref[...], normal, scale)


SMEM = pl.BlockSpec(memory_space=pltpu.SMEM)
VMEM = pl.BlockSpec(memory_space=pltpu.VMEM)
ANY = pl.BlockSpec(memory_space=pl.ANY)


def call(kernel, name, smem, anys, vmem, out_any, out_vmem, scratch):
    return pl.pallas_call(
        kernel,
        name=name,
        out_shape=tuple(out_any) + tuple(out_vmem),
        in_specs=[SMEM] * len(smem) + [ANY] * len(anys) + [VMEM] * len(vmem),
        out_specs=tuple([ANY] * len(out_any) + [VMEM] * len(out_vmem)),
        scratch_shapes=scratch,
        compiler_params=pltpu.CompilerParams(vmem_limit_bytes=VMEM_LIMIT),
    )(*smem, *anys, *vmem)


def shaped(*shape, kind=BF):
    return jax.ShapeDtypeStruct(shape, kind)


def shift(ways, step):
    return [(i, (i + step) % ways) for i in range(ways)]


CORE, X_BIT, Y_BIT = 1, 2, 4


def routes(ways):
    first = [(f, f ^ (Y_BIT if f & CORE else X_BIT)) for f in range(ways)]
    second = [(f, f ^ (X_BIT if f & CORE else Y_BIT)) for f in range(ways)]
    core = [(f, f ^ CORE) for f in range(ways)]
    return first, second, core


def owners(ways):
    if ways != PIECES:
        return jnp.arange(PIECES, dtype=jnp.int32)
    f = lax.axis_index("fsdp")
    odd = f % 2 == 1
    one = jnp.where(odd, Y_BIT, X_BIT)
    two = jnp.where(odd, X_BIT, Y_BIT)
    return jnp.stack(
        [f, f ^ one, f ^ two, f ^ 6, f ^ 1, f ^ 1 ^ two, f ^ 1 ^ one, f ^ 7]
    ).astype(jnp.int32)


def gather_weights(block, fsdp, tp):
    if fsdp != PIECES:
        block = lax.all_gather(block, "fsdp", axis=0, tiled=True)
    near = jnp.stack([block] + [lax.ppermute(block, "tp", shift(tp, s)) for s in range(1, tp)])
    if fsdp != PIECES:
        return jnp.split(near, PIECES, axis=1)
    first, second, core = routes(fsdp)
    one = lax.ppermute(near, "fsdp", first)
    two = lax.ppermute(near, "fsdp", second)
    far = lax.ppermute(one, "fsdp", second)
    mine = [near, one, two, far]
    return mine + [lax.ppermute(piece, "fsdp", core) for piece in mine]


def added(left, right):
    return (left.astype(F32) + right.astype(F32)).astype(BF)


def scatter_grads(pieces, fsdp, tp):
    if fsdp != PIECES:
        whole = jnp.concatenate(pieces, axis=1)
        part = lax.psum_scatter(whole, "fsdp", scatter_dimension=1, tiled=True)
    else:
        first, second, core = routes(fsdp)
        got = [added(a, lax.ppermute(b, "fsdp", core)) for a, b in zip(pieces[:4], pieces[4:])]
        near = added(got[0], lax.ppermute(got[2], "fsdp", second))
        one = added(got[1], lax.ppermute(got[3], "fsdp", second))
        part = added(near, lax.ppermute(one, "fsdp", first))
    total = part[0].astype(F32)
    for s in range(1, tp):
        total = total + lax.ppermute(part[s], "tp", shift(tp, -s)).astype(F32)
    return total


def gather_gains(gains, fsdp):
    if fsdp != PIECES:
        return lax.all_gather(gains, "fsdp", axis=1, tiled=True).astype(F32)
    f = lax.axis_index("fsdp")
    parts = [gains] + [
        lax.ppermute(gains, "fsdp", [(i, i ^ r) for i in range(fsdp)]) for r in range(1, fsdp)
    ]
    spread = jnp.take(jnp.stack(parts), jnp.arange(fsdp) ^ f, axis=0).astype(F32)
    return jnp.swapaxes(spread, 0, 1).reshape(gains.shape[0], -1)


def sum_gains(grads, fsdp, tp):
    if fsdp != PIECES:
        grads = lax.psum(grads, ("fsdp", "tp"))
    else:
        for bit in (CORE, X_BIT, Y_BIT):
            grads = grads + lax.ppermute(grads, "fsdp", [(i, i ^ bit) for i in range(fsdp)])
        for bit in (1, 2):
            grads = grads + lax.ppermute(grads, "tp", [(i, i ^ bit) for i in range(tp)])
    rows = grads.shape[1] // fsdp
    return lax.dynamic_slice_in_dim(grads, lax.axis_index("fsdp") * rows, rows, axis=1)


def on_device(
    fsdp,
    tp,
    hidden_in,
    memory,
    seg_lengths,
    seg_parents,
    path_pos,
    self_query,
    self_key,
    self_value,
    self_output,
    attn_gain,
    cross_query,
    cross_key,
    cross_value,
    cross_output,
    cross_gain,
    gate_weight,
    up_weight,
    down_weight,
    feed_gain,
    out_grad,
):
    rows, model = hidden_in.shape
    mem_rows = memory.shape[0]
    per_tree = tp // seg_lengths.shape[0]
    t_index = lax.axis_index("tp")
    pair = [(i, i ^ 1) for i in range(tp)]
    width = self_query.shape[1]
    hidden = gate_weight.shape[1]
    eighth = model // PIECES

    gains = gather_gains(jnp.stack([attn_gain, cross_gain, feed_gain]), fsdp)
    other = lax.ppermute(hidden_in, "tp", pair)
    first = gather_weights(jnp.concatenate([self_key, self_value, self_query], axis=1), fsdp, tp)
    mem_all = jnp.concatenate([memory, lax.ppermute(memory, "tp", pair)], axis=0)
    second = gather_weights(
        jnp.concatenate(
            [cross_key, cross_value, self_output.T, cross_query, cross_output.T], axis=1
        ),
        fsdp,
        tp,
    )
    third = gather_weights(
        jnp.concatenate([gate_weight, up_weight, down_weight.T], axis=1), fsdp, tp
    )
    gain_one, gain_two, gain_three = gains[0:1], gains[1:2], gains[2:3]
    meta = jnp.concatenate(
        [
            owners(fsdp),
            jnp.stack([t_index // per_tree, t_index % per_tree]).astype(jnp.int32),
        ]
    )
    dma = pltpu.SemaphoreType.DMA
    keys = 2 * rows
    mems = 2 * mem_rows
    lanes = -(-width // 128) * 128

    mixed, kv, query, lse = call(
        functools.partial(self_forward_kernel, pl.ds(0, 3 * width)),
        "self_forward",
        (meta, seg_lengths, seg_parents),
        first,
        (hidden_in, other, gain_one),
        (),
        (
            shaped(tp, rows, width),
            shaped(tp, keys, 2 * width),
            shaped(tp, rows, width),
            shaped(tp, rows, 128, kind=F32),
        ),
        [
            pltpu.VMEM((tp, model, 3 * width), BF),
            pltpu.VMEM((keys, model), BF),
            pltpu.VMEM((rows, 128), BF),
            pltpu.VMEM((keys, 128), BF),
            dma((tp, PIECES)),
        ],
    )
    after_attn, after_cross, mixed_two, query_two, kv_two, lse_two = call(
        functools.partial(cross_forward_kernel, pl.ds(0, 5 * width)),
        "cross_forward",
        (meta,),
        second,
        (hidden_in, mixed, mem_all, gain_two),
        (),
        (
            shaped(rows, model, kind=F32),
            shaped(rows, model, kind=F32),
            shaped(tp, rows, width),
            shaped(tp, rows, width),
            shaped(tp, mems, 2 * width),
            shaped(tp, rows, 128, kind=F32),
        ),
        [
            pltpu.VMEM((tp, model, 5 * width), BF),
            pltpu.VMEM((rows, model), BF),
            dma((tp, PIECES)),
        ],
    )
    *feed_grads, layer_out, grad_after_cross, dgain_three = call(
        functools.partial(feed_kernel, pl.ds(0, 3 * hidden)),
        "feed",
        (meta,),
        third,
        (after_cross, out_grad, gain_three),
        [shaped(tp, eighth, 3 * hidden)] * PIECES,
        (
            shaped(rows, model),
            shaped(rows, model, kind=F32),
            shaped(1, model, kind=F32),
        ),
        [
            pltpu.VMEM((tp, model, 3 * hidden), BF),
            pltpu.VMEM((rows, model), BF),
            pltpu.VMEM((model, rows), BF),
            pltpu.VMEM((model, rows), BF),
            pltpu.VMEM((rows, model), F32),
            pltpu.VMEM((rows, model), F32),
            pltpu.VMEM((2, model, 3 * hidden), BF),
            dma((tp, PIECES)),
            dma((2, PIECES)),
        ],
    )
    owned_feed = scatter_grads(feed_grads, fsdp, tp)
    *cross_grads, grad_after_attn, dmem, dgain_two = call(
        functools.partial(cross_backward_kernel, pl.ds(0, 5 * width)),
        "cross_backward",
        (meta,),
        second,
        (
            grad_after_cross,
            after_attn,
            mem_all,
            gain_two,
            mixed_two,
            query_two,
            kv_two,
            lse_two,
        ),
        [shaped(tp, eighth, 4 * width)] * PIECES,
        (
            shaped(rows, model, kind=F32),
            shaped(mems, model),
            shaped(1, model, kind=F32),
        ),
        [
            pltpu.VMEM((tp, model, 5 * width), BF),
            pltpu.VMEM((model, rows), BF),
            pltpu.VMEM((rows, model), BF),
            pltpu.VMEM((model, rows), BF),
            pltpu.VMEM((model, mems), BF),
            pltpu.VMEM((rows, model), F32),
            pltpu.VMEM((mems, model), F32),
            pltpu.VMEM((rows, width), BF),
            pltpu.VMEM((mems, 2 * width), BF),
            pltpu.VMEM((2, model, 4 * width), BF),
            dma((tp, PIECES)),
            dma((2, PIECES)),
        ],
    )
    owned_cross = scatter_grads(cross_grads, fsdp, tp)
    memory_grad = dmem[:mem_rows].astype(F32) + lax.ppermute(dmem[mem_rows:], "tp", pair).astype(
        F32
    )
    *self_grads, back, away, dgain_one = call(
        functools.partial(
            self_backward_kernel, pl.ds(0, 3 * width), pl.ds(2 * width, lanes)
        ),
        "self_backward",
        (meta, seg_lengths, seg_parents),
        list(first) + list(second),
        (grad_after_attn, hidden_in, other, gain_one, mixed, query, kv, lse),
        [shaped(tp, eighth, 4 * width)] * PIECES,
        (
            shaped(rows, model, kind=F32),
            shaped(rows, model),
            shaped(1, model, kind=F32),
        ),
        [
            pltpu.VMEM((tp, model, 3 * width), BF),
            pltpu.VMEM((tp, model, lanes), BF),
            pltpu.VMEM((model, keys), BF),
            pltpu.VMEM((rows, model), BF),
            pltpu.VMEM((model, rows), BF),
            pltpu.VMEM((keys, model), F32),
            pltpu.VMEM((rows, width), BF),
            pltpu.VMEM((keys, 2 * width), BF),
            pltpu.VMEM((rows, 128), BF),
            pltpu.VMEM((keys, 128), BF),
            pltpu.VMEM((2, model, 4 * width), BF),
            dma((tp, PIECES)),
            dma((tp, PIECES)),
            dma((2, PIECES)),
        ],
    )
    came = lax.ppermute(away, "tp", pair)
    owned_self = scatter_grads(self_grads, fsdp, tp)
    owned_gains = sum_gains(
        jnp.concatenate([dgain_one, dgain_two, dgain_three], axis=0), fsdp, tp
    )
    (input_grad,) = call(
        finish_kernel,
        "finish",
        (),
        (),
        (grad_after_attn, hidden_in, back, came, gain_one),
        (),
        (shaped(rows, model, kind=F32),),
        [],
    )
    return (
        layer_out,
        input_grad,
        memory_grad,
        owned_self[:, 2 * width : 3 * width],
        owned_self[:, :width],
        owned_self[:, width : 2 * width],
        owned_self[:, 3 * width :].T,
        owned_gains[0],
        owned_cross[:, 2 * width : 3 * width],
        owned_cross[:, :width],
        owned_cross[:, width : 2 * width],
        owned_cross[:, 3 * width :].T,
        owned_gains[1],
        owned_feed[:, :hidden],
        owned_feed[:, hidden : 2 * hidden],
        owned_feed[:, 2 * hidden :].T,
        owned_gains[2],
    )


def solution(mesh):
    rows = P(("fsdp", "tp"), None)
    inward = P("fsdp", "tp")
    outward = P("tp", "fsdp")
    vector = P("fsdp")
    trees = P("fsdp", None)
    in_specs = (
        (rows, rows, trees, trees, vector)
        + (inward, inward, inward, outward, vector) * 2
        + (inward, inward, outward, vector, rows)
    )
    out_specs = (
        (rows, rows, rows)
        + (inward, inward, inward, outward, vector) * 2
        + (inward, inward, outward, vector)
    )
    body = functools.partial(on_device, mesh.shape["fsdp"], mesh.shape["tp"])
    return jax.shard_map(
        body, mesh=mesh, in_specs=in_specs, out_specs=out_specs, check_vma=False
    )
```
